32 devices in a mesh: blk: 8 (over y, x, core), pair: 4 (over z).
Axes of the slice: x: 2, y: 2, z: 4, core: 2. Of those that a mesh axis runs over, the one named last changes fastest.
Arguments:
- half_blocks: bfloat16 [1024, 32, 256], P('blk', 'pair'), may hold values from -6 to 6
- row_target: int32 [1024], P('blk'), may hold values from 0 to 1023, as said below
- vir_coeff: bfloat16 [256, 128], replicated, may hold values from -0.375 to 0.375
- occ_energy: float32 [32], replicated, may hold values from -2 to -0.3
- vir_energy: float32 [128], replicated, may hold values from 0.1 to 3
- freq_pick: int32 [6], replicated, may hold values from 0 to 31
Outputs:
- response: float32 [6, 1024, 1024], P(None, 'blk', 'pair')
The draws below stay inside these ranges and needn't reach their ends.
Inputs may be any that keep to these rules, and one draw needn't show every extreme that they name: row_target is a permutation of the auxiliary functions. The rows of one device go at most 32 to the block of 128 functions of any one owner; every device sends exactly 32 rows to some owner, and every owner receives exactly 32 rows from some device. All devices send the same counts of rows, to owners paired in different ways.
All inputs are finite; a program needn't handle non-finite values.
Results may differ from the reference program's by a relative error of at most 0.0024.
Values may be sent and summed in bfloat16 or wider, within the bound.
No kernel may reach another device: no remote copies, remote signals or barrier semaphores. Data moves between devices by JAX's collectives and lax.ppermute only.
A program may use at most 64 MiB of HBM per device.

```python
import math
import jax
import jax.numpy as jnp
from jax import lax

NBAS = 256
NVIR = 128
ROWS = 128
NFREQ = 6
STOPS = 8
GRID = 32
CAP = 32
NAUX = 1024
NOCC = 32


def draw_row_target(key, part):
    count = NAUX // ROWS
    shuffled = jax.random.permutation(jax.random.fold_in(key, 11), CAP * count)
    position = jnp.argsort(shuffled).astype(jnp.int32)
    busiest = jax.random.randint(jax.random.fold_in(key, 12), (), 0, count)
    slot_ids = jnp.arange(CAP * count, dtype=jnp.int32)
    priority = jnp.where(slot_ids // CAP == busiest, -1, position)
    chosen = jnp.argsort(priority)[:ROWS].astype(jnp.int32)
    offsets = jnp.sort(chosen // CAP)
    owner_perm = jax.random.permutation(jax.random.fold_in(key, 13), count)
    source_perm = jax.random.permutation(jax.random.fold_in(key, 14), count)
    source = jnp.arange(count, dtype=jnp.int32)[:, None]
    owners = owner_perm[(source_perm[source] + offsets[None, :]) % count]
    slot_perm = jax.vmap(lambda subkey: jax.random.permutation(subkey, ROWS))(jax.random.split(jax.random.fold_in(key, 15), count))
    landing = slot_perm[owners, jnp.arange(ROWS, dtype=jnp.int32)[None, :]]
    target = owners * ROWS + landing
    shuffle = jax.vmap(lambda subkey: jax.random.permutation(subkey, ROWS))(jax.random.split(jax.random.fold_in(key, 16), count))
    placed = jnp.zeros((count, ROWS), jnp.int32).at[source, shuffle].set(target.astype(jnp.int32))
    return placed.reshape(NAUX).astype(jnp.int32)


def place_ends(array, key, least, largest):
    dims = array.shape
    spot = [jax.random.randint(jax.random.fold_in(key, axis), (), 0, dims[axis]) for axis in range(len(dims))]
    array = array.at[tuple(spot)].set(least)
    longest = dims.index(max(dims))
    spot[longest] = (spot[longest] + 1) % dims[longest]
    return array.at[tuple(spot)].set(largest)


def shard_levels(key, dims, shards, smallest, top_value):
    def one(dim, parts):
        steps = jax.random.uniform(jax.random.fold_in(jax.random.fold_in(key, 6), dim), (parts,), jnp.float32, smallest / len(shards), top_value / len(shards))
        return jnp.repeat(jnp.exp(steps), dims[dim] // parts).reshape((-1,) + (1,) * (len(dims) - dim - 1))

    level = one(*shards[0])
    for cut in shards[1:]:
        level = level * one(*cut)
    return level


def gaussian(key, extent, deviation, reach, shards=(), kind=jnp.bfloat16):
    level = shard_levels(key, extent, shards, -0.22, 0.18) if shards else 1.0
    values = jax.random.normal(key, extent, jnp.float32) * deviation * level
    return jnp.minimum(jnp.maximum(values, -reach), reach).astype(kind)


def setup_inputs(seed: int = 0) -> dict:
    arg_keys = jax.random.split(jax.random.key(seed), 7)
    half_blocks = gaussian(arg_keys[0], (NAUX, NOCC, NBAS), 1.0, 6.0, ((0, 8), (1, 4)))
    row_target = draw_row_target(jax.random.fold_in(arg_keys[6], 71), 0)
    vir_coeff = gaussian(arg_keys[2], (NBAS, NVIR), NBAS ** -0.5, 0.375)
    occ_energy = jnp.clip(jax.random.uniform(arg_keys[3], (NOCC,), jnp.float32, -2.0, -0.3), -2.0, -0.3)
    vir_energy = jnp.clip(jax.random.uniform(arg_keys[4], (NVIR,), jnp.float32, 0.1, 3.0), 0.1, 3.0)
    freq_pick = place_ends(jax.random.randint(arg_keys[5], (NFREQ,), 0, GRID), jax.random.fold_in(arg_keys[5], 1), 0, GRID - 1).astype(jnp.int32)
    return {"half_blocks": half_blocks, "row_target": row_target, "vir_coeff": vir_coeff, "occ_energy": occ_energy, "vir_energy": vir_energy, "freq_pick": freq_pick}


def response_factor(occ_values, vir_values, frequency):
    energy_gap = vir_values[None, :] - occ_values[:, None]
    factor = 2.0 * energy_gap[None] / (energy_gap[None] * energy_gap[None] + frequency[:, None, None] * frequency[:, None, None])
    return factor.reshape(frequency.shape[0], -1)

def reference(half_blocks, row_target, vir_coeff, occ_energy, vir_energy, freq_pick):
    aux_count, occ_count, basis = half_blocks.shape
    virtual = vir_coeff.shape[1]
    placed = jnp.zeros_like(half_blocks).at[row_target].set(half_blocks)
    vir_blocks = jnp.dot(placed.reshape(aux_count * occ_count, basis), vir_coeff, preferred_element_type=jnp.float32)
    vir_blocks = vir_blocks.astype(jnp.bfloat16).reshape(aux_count, occ_count * virtual)
    frequency = 0.5 * jnp.tan(jnp.pi * (freq_pick.astype(jnp.float32) + 0.5) / (2.0 * GRID))
    factor = response_factor(occ_energy, vir_energy, frequency)
    block_count = aux_count // ROWS
    lowest = STOPS // 2 - 1
    scaling = 1.0 / math.sqrt(occ_count * virtual)
    grouped = vir_blocks.reshape(block_count, ROWS, occ_count * virtual)

    def one_block(block_id):
        row_block = lax.dynamic_slice_in_dim(vir_blocks, block_id * ROWS, ROWS, 0)
        weighted = (row_block.astype(jnp.float32)[None] * factor[:, None, :]).astype(jnp.bfloat16)
        partner_ids = ((block_id + jnp.arange(STOPS, dtype=jnp.int32) - lowest) % block_count).astype(jnp.int32)
        partners = jnp.take(grouped, partner_ids, axis=0).reshape(STOPS * ROWS, occ_count * virtual)
        tiles = lax.dot_general(weighted.reshape(NFREQ * ROWS, -1).astype(jnp.float32), partners.astype(jnp.float32), (((1,), (1,)), ((), ())), precision=lax.Precision.HIGHEST)
        return tiles.reshape(NFREQ, ROWS, STOPS * ROWS) * scaling
    result = lax.map(one_block, jnp.arange(block_count, dtype=jnp.int32))
    return jnp.transpose(result, (1, 0, 2, 3)).reshape(NFREQ, aux_count, STOPS * ROWS)
```

```python
import math

import jax
import jax.numpy as jnp
from jax import lax
from jax.experimental import pallas as pl
from jax.experimental.pallas import tpu as pltpu
from jax.sharding import PartitionSpec as P

STOPS = 8
GRID = 32
LOWEST = STOPS // 2 - 1
ID_ROWS = 16


def from_behind(x, axis, by):
    devices = lax.axis_size(axis)
    return lax.ppermute(x, axis, [(i, (i + by) % devices) for i in range(devices)])


def swap(x, axis, mask):
    devices = lax.axis_size(axis)
    return lax.ppermute(x, axis, [(i, i ^ mask) for i in range(devices)])


def response_factor(occ_values, vir_values, frequency):
    energy_gap = vir_values[None, :] - occ_values[:, None]
    factor = (
        2.0
        * energy_gap[None]
        / (
            energy_gap[None] * energy_gap[None]
            + frequency[:, None, None] * frequency[:, None, None]
        )
    )
    return factor.reshape(frequency.shape[0], -1)


def to_virtual(blocks, coeff):
    row_count, occ_count, basis = blocks.shape
    product = jnp.dot(
        blocks.reshape(row_count * occ_count, basis), coeff, preferred_element_type=jnp.float32
    )
    return product.astype(jnp.bfloat16).reshape(row_count, occ_count * coeff.shape[1])


def frequencies(freq_pick):
    return 0.5 * jnp.tan(jnp.pi * (freq_pick.astype(jnp.float32) + 0.5) / (2.0 * GRID))


def put_rows(arrived, arrived_ids, row_count):
    safe_ids = jnp.where(arrived_ids >= 0, arrived_ids, row_count)
    empty = jnp.zeros((row_count, arrived.shape[1]), arrived.dtype)
    return empty.at[safe_ids].set(arrived, mode="drop")


def routed_shards(half_blocks, row_target, vir_coeff, occ_energy, vir_energy, freq_pick):
    blk_count = lax.axis_size("blk")
    row_count, occ_dev, _ = half_blocks.shape
    virtual = vir_coeff.shape[1]
    capacity = min(row_count, 2 * max(1, row_count // blk_count))
    owners = row_target // row_count
    onehot = (owners[:, None] == jnp.arange(blk_count, dtype=jnp.int32)[None, :]).astype(jnp.int32)
    earlier = jnp.cumsum(onehot, axis=0) - onehot
    position = owners * capacity + jnp.sum(earlier * onehot, axis=1)
    landing = (
        jnp.full((blk_count * capacity,), -1, jnp.int32).at[position].set(row_target % row_count)
    )
    payload = to_virtual(half_blocks, vir_coeff)
    outgoing = (
        jnp.zeros((blk_count * capacity, payload.shape[1]), jnp.bfloat16).at[position].set(payload)
    )
    arrived, arrived_ids = (
        lax.all_to_all(outgoing, "blk", split_axis=0, concat_axis=0, tiled=True),
        lax.all_to_all(landing, "blk", split_axis=0, concat_axis=0, tiled=True),
    )
    virt_rows = put_rows(arrived, arrived_ids, row_count)
    frequency = frequencies(freq_pick)
    scaling = 1.0 / math.sqrt(occ_energy.shape[0] * virtual)
    freq_count = frequency.shape[0]
    upper = [virt_rows]
    current = virt_rows
    for stop in range(STOPS - 1 - LOWEST):
        current = from_behind(current, "blk", -1)
        upper.append(current)
    lower = []
    current = virt_rows
    for stop in range(LOWEST):
        current = from_behind(current, "blk", 1)
        lower.append(current)
    pieces = lower[::-1] + upper
    own_occ = lax.dynamic_slice_in_dim(occ_energy, lax.axis_index("pair") * occ_dev, occ_dev)
    factor = response_factor(own_occ, vir_energy, frequency)
    weighted = (virt_rows.astype(jnp.float32)[None] * factor[:, None, :]).astype(jnp.bfloat16)
    partners = jnp.concatenate(pieces, axis=0)
    tiles = lax.dot_general(
        weighted.reshape(freq_count * row_count, -1),
        partners,
        (((1,), (1,)), ((), ())),
        preferred_element_type=jnp.float32,
    )
    summed = lax.psum_scatter(
        tiles.reshape(freq_count, row_count, -1), "pair", scatter_dimension=2, tiled=True
    )
    return summed * scaling


VMEM = pl.BlockSpec(memory_space=pltpu.VMEM)
SMEM = pl.BlockSpec(memory_space=pltpu.SMEM)


def kernel_call(body, out_shape, flops, moved, operands, in_specs, scratch=(), aliases={}):
    return pl.pallas_call(
        body,
        out_shape=out_shape,
        in_specs=in_specs,
        out_specs=jax.tree.map(lambda _: VMEM, out_shape),
        scratch_shapes=scratch,
        input_output_aliases=aliases,
        cost_estimate=pl.CostEstimate(flops=flops, bytes_accessed=moved, transcendentals=0),
        compiler_params=pltpu.CompilerParams(vmem_limit_bytes=30 * 2**20),
    )(*operands)


def pick_rows(wanted_ref, id_refs, piece_refs, rows):
    wanted = [
        wanted_ref[q] * rows + lax.broadcasted_iota(jnp.int32, (rows, rows), 0)
        for q in range(wanted_ref.shape[0])
    ]
    wanted = jnp.concatenate(wanted, axis=0).astype(jnp.float32)
    total = None
    for at in range(0, len(piece_refs), 2):
        chosen = []
        for ids in id_refs[at : at + 2]:
            digits = ids[...].astype(jnp.float32)
            number = digits[0:1, :rows] * rows + digits[1:2, :rows]
            chosen.append(jnp.where(wanted == number, 1.0, 0.0).astype(jnp.bfloat16))
        held = jnp.concatenate([p[:rows, :] for p in piece_refs[at : at + 2]], axis=0)
        part = jnp.dot(
            jnp.concatenate(chosen, axis=1), held, preferred_element_type=jnp.float32
        )
        total = part if total is None else total + part
    return total


def weigh(row_block, factor, rows):
    wide = row_block.astype(jnp.float32)
    return jnp.concatenate(
        [(wide * factor[k : k + 1, :]).astype(jnp.bfloat16) for k in range(factor.shape[0])], axis=0
    )


def contract(left, right):
    return lax.dot_general(
        left, right, (((1,), (1,)), ((), ())), preferred_element_type=jnp.float32
    )


def place_kernel(count, rows, *refs):
    wanted, ids, pieces, placed = refs[0], refs[1 : 1 + count], refs[1 + count : 1 + 2 * count], refs[-1]
    placed[...] = pick_rows(wanted, ids, pieces, rows).astype(jnp.bfloat16)


def first_kernel(rows, cols, factor, placed, local, remote):
    weighted = weigh(placed[:rows, :], factor[...], rows)
    local[...] = contract(weighted, placed[rows : rows + cols, :])
    remote[...] = contract(weighted, placed[rows + cols :, :])


def second_kernel(count, rows, cols, *refs):
    wanted, ids, pieces = refs[0], refs[1 : 1 + count], refs[1 + count : 1 + 2 * count]
    early, factor, remote_before, away, placed, weighted = refs[1 + 2 * count :]
    placed[...] = (
        pick_rows(wanted, ids, pieces, rows) + early[...].astype(jnp.float32)
    ).astype(jnp.bfloat16)
    weighted[...] = weigh(placed[:rows, :], factor[...], rows)
    total = remote_before[...] + contract(weighted[...], placed[rows + cols :, :])
    away[...] = total.astype(jnp.bfloat16)


def local_kernel(rows, cols, placed, weighted, before, after):
    after[...] = before[...] + contract(weighted[...], placed[rows : rows + cols, :])


def final_kernel(scaling, rows, mine, theirs, out):
    for k in range(out.shape[0]):
        at = slice(k * rows, (k + 1) * rows)
        out[k] = (mine[at, :] + theirs[at, :].astype(jnp.float32)) * scaling


def gathered_shards(half_blocks, row_target, vir_coeff, occ_energy, vir_energy, freq_pick):
    blk_count, pair_count = lax.axis_size("blk"), lax.axis_size("pair")
    rows, occ_dev, _ = half_blocks.shape
    virtual = vir_coeff.shape[1]
    depth = occ_dev * virtual
    freq_count = freq_pick.shape[0]
    scaling = 1.0 / math.sqrt(occ_energy.shape[0] * virtual)
    per_pair = STOPS // pair_count
    cols = per_pair * rows
    blk, pair = lax.axis_index("blk"), lax.axis_index("pair")
    far, near = pair_count // 2, 1
    core, across, along = 1, 2, 4

    own = to_virtual(half_blocks, vir_coeff)
    digits = jnp.stack([row_target // rows, row_target % rows]).astype(jnp.bfloat16)
    digits = jnp.pad(digits, ((0, ID_ROWS - 2), (0, depth - rows)))
    tagged = jnp.concatenate([own, digits], axis=0)

    other = swap(own, "pair", far)
    beside = swap(tagged, "blk", across)
    above = swap(tagged, "blk", along)
    corner = swap(tagged, "blk", across | along)
    mine = [tagged, beside, above, corner]
    first = []
    for piece in mine:
        first += [piece, swap(piece, "blk", core)]

    half = rows // 2
    other_beside = swap(other, "blk", across)
    other_above = swap(other, "blk", along)
    corner_low = swap(other_above[:half], "blk", across)
    corner_high = swap(other_beside[half:], "blk", along)

    frequency = frequencies(freq_pick)

    def slice_factor(index):
        occ = lax.dynamic_slice_in_dim(occ_energy, index * occ_dev, occ_dev)
        return response_factor(occ, vir_energy, frequency)

    ids = [piece[rows:, :] for piece in first]
    local_from, remote_from = pair * per_pair, (pair ^ near) * per_pair
    steps = [local_from + s for s in range(per_pair)] + [remote_from + s for s in range(per_pair)]
    wanted = jnp.stack([blk] + [(blk + s - LOWEST) % blk_count for s in steps]).astype(jnp.int32)
    wanted_rows = wanted.shape[0] * rows

    def shaped(count, width, kind):
        return jax.ShapeDtypeStruct((count, width), kind)

    placed_first = kernel_call(
        lambda *refs: place_kernel(8, rows, *refs),
        shaped(wanted_rows, depth, jnp.bfloat16),
        2 * wanted_rows * 8 * rows * depth, 8 * rows * depth * 2,
        [wanted] + ids + first, [SMEM] + [VMEM] * 16,
    )
    tile = shaped(freq_count * rows, cols, jnp.float32)
    local, remote = kernel_call(
        lambda *refs: first_kernel(rows, cols, *refs),
        (tile, tile), 4 * freq_count * rows * cols * depth, wanted_rows * depth * 2,
        [slice_factor(pair), placed_first], [VMEM] * 2,
    )

    early = []
    for piece in (other, other_beside, other_above):
        early += [piece, swap(piece, "blk", core)]
    placed_early = kernel_call(
        lambda *refs: place_kernel(6, rows, *refs),
        shaped(wanted_rows, depth, jnp.bfloat16),
        2 * wanted_rows * 6 * rows * depth, 6 * rows * depth * 2,
        [wanted] + ids[:6] + early, [SMEM] + [VMEM] * 12,
    )
    late = jnp.concatenate([corner_low, corner_high], axis=0)
    late = [late, swap(late, "blk", core)]
    away, placed_last, weighted = kernel_call(
        lambda *refs: second_kernel(2, rows, cols, *refs),
        (
            shaped(freq_count * rows, cols, jnp.bfloat16),
            shaped(wanted_rows, depth, jnp.bfloat16),
            shaped(freq_count * rows, depth, jnp.bfloat16),
        ),
        2 * wanted_rows * 2 * rows * depth + 2 * freq_count * rows * cols * depth,
        wanted_rows * depth * 2,
        [wanted] + ids[6:] + late + [placed_early, slice_factor(pair ^ far), remote],
        [SMEM] + [VMEM] * 7,
    )
    theirs = swap(away, "pair", near)
    local = kernel_call(
        lambda *refs: local_kernel(rows, cols, *refs),
        tile, 2 * freq_count * rows * cols * depth, freq_count * rows * depth * 2,
        [placed_last, weighted, local], [VMEM] * 3, aliases={2: 0},
    )
    return kernel_call(
        lambda *refs: final_kernel(scaling, rows, *refs),
        jax.ShapeDtypeStruct((freq_count, rows, cols), jnp.float32),
        freq_count * rows * cols * 2, freq_count * rows * cols * 10,
        [local, theirs], [VMEM] * 2,
    )


def solution(mesh):
    covers = mesh.shape["blk"] == STOPS and mesh.shape["pair"] == STOPS // 2
    return jax.shard_map(
        gathered_shards if covers else routed_shards,
        mesh=mesh,
        in_specs=(P("blk", "pair", None), P("blk"), P(), P(), P(), P()),
        out_specs=P(None, "blk", "pair"),
        check_vma=False,
    )
```
